256 devices in a mesh: dp: 16 (over z, core), mp: 16 (over y, x).
Axes of the slice: x: 4, y: 4, z: 8, core: 2. Of those that a mesh axis runs over, the one named last changes fastest.
Arguments:
- candidates: bfloat16 [4096, 4096], P('dp', 'mp'), may hold values from -6 to 6
- hold_gate: bfloat16 [4096, 8192], P(None, 'mp'), may hold values from -0.09375 to 0.09375
- hold_up: bfloat16 [4096, 8192], P(None, 'mp'), may hold values from -0.09375 to 0.09375
- probe: float32 [8192], P('mp'), as said below
- chosen: int32 [16, 192], replicated, may hold values from 0 to 4095, as said below
- counts: int32 [16], replicated, may hold values from 24 to 192, as said below
- gate_w: bfloat16 [4096, 14336], P('dp', 'mp'), may hold values from -0.09375 to 0.09375
- up_w: bfloat16 [4096, 14336], P('dp', 'mp'), may hold values from -0.09375 to 0.09375
- cotangent: bfloat16 [3072, 14336], P('dp', 'mp'), may hold values from -6 to 6
Outputs:
- grad_gate: bfloat16 [4096, 14336], P('dp', 'mp')
- grad_up: bfloat16 [4096, 14336], P('dp', 'mp')
- hidden: bfloat16 [3072, 14336], P('dp', 'mp')
- cand_weight: float32 [4096], P('dp')
The draws below stay inside these ranges and needn't reach their ends.
Inputs may be any that keep to these rules, and one draw needn't show every extreme that they name: `chosen`: all entries are distinct candidate indices. `counts`: exactly one training shard uses all 192 slots in every draw. `probe`: magnitudes at most 12 / sqrt(8192).
All inputs are finite; a program needn't handle non-finite values.
Results may differ from the reference program's by a relative error of at most 0.0057.
Values may be sent and summed in bfloat16 or wider, within the bound.
A program may use at most 128 MiB of HBM per device.

```python
import math
import jax
import jax.numpy as jnp

D = 4096
HOLD_FF = 8192
TRAIN_FF = 14336
CAND_DEV = 256
CAP = 192
CAND = 4096
TRAIN_SHARDS = 16
ROWS = 3072


def draw_probe(key, part):
    base = jnp.clip(jax.random.normal(key, (HOLD_FF,), jnp.float32), -4.0, 4.0)
    ramp = jnp.exp(math.log(3.0) * jnp.arange(HOLD_FF, dtype=jnp.float32) / HOLD_FF)
    return base * ramp * HOLD_FF ** (-0.5)


def draw_chosen(key, part):
    key_perm = jax.random.fold_in(key, 37)
    key_offs = jax.random.fold_in(key, 41)
    orders = jax.vmap(lambda k: jax.random.permutation(k, CAND_DEV))(jax.random.split(key_perm, TRAIN_SHARDS))
    offsets = jax.random.randint(key_offs, (CAP,), 0, TRAIN_SHARDS)
    offsets = jnp.where(jnp.arange(CAP) == 0, 0, offsets)
    shard_ids = jnp.arange(TRAIN_SHARDS)[:, None]
    slot_ids = jnp.arange(CAP)[None, :]
    source = (shard_ids + TRAIN_SHARDS // 2 + offsets[None, :]) % TRAIN_SHARDS
    local = orders[source, slot_ids]
    return (source * CAND_DEV + local).astype(jnp.int32)


def draw_counts(key, part):
    key_base = jax.random.fold_in(key, 11)
    key_top = jax.random.fold_in(key, 23)
    base = jax.random.randint(key_base, (TRAIN_SHARDS,), CAP // 8, CAP // 2 + 1)
    busiest = jax.random.randint(key_top, (), 0, TRAIN_SHARDS)
    return jnp.where(jnp.arange(TRAIN_SHARDS) == busiest, CAP, base).astype(jnp.int32)


def shard_levels(own_key, extent, cuts, low, top_value):
    def one(position, shards_of):
        steps = jax.random.uniform(jax.random.fold_in(jax.random.fold_in(own_key, 6), position), (shards_of,), jnp.float32, low / len(cuts), top_value / len(cuts))
        return jnp.repeat(jnp.exp(steps), extent[position] // shards_of).reshape((-1,) + (1,) * (len(extent) - position - 1))

    level = one(*cuts[0])
    for cut in cuts[1:]:
        level = level * one(*cut)
    return level


def normal_values(own_key, extent, spread, most, pieces=(), kind=jnp.bfloat16):
    factor_of = shard_levels(own_key, extent, pieces, -0.22, 0.18) if pieces else 1.0
    array = jax.random.normal(own_key, extent, jnp.float32) * spread * factor_of
    return jnp.minimum(jnp.maximum(array, -most), most).astype(kind)


def setup_inputs(seed: int = 0) -> dict:
    key_list = jax.random.split(jax.random.key(seed), 10)
    return {
        "candidates": normal_values(key_list[0], (CAND, D), 1.0, 6.0, ((0, 16), (1, 16))),
        "hold_gate": normal_values(key_list[1], (D, HOLD_FF), D ** -0.5, 0.09375, ((1, 16),)),
        "hold_up": normal_values(key_list[2], (D, HOLD_FF), D ** -0.5, 0.09375, ((1, 16),)),
        "probe": draw_probe(jax.random.fold_in(key_list[9], 71), 0),
        "chosen": draw_chosen(jax.random.fold_in(key_list[9], 71), 0),
        "counts": draw_counts(jax.random.fold_in(key_list[9], 71), 0),
        "gate_w": normal_values(key_list[6], (D, TRAIN_FF), D ** -0.5, 0.09375, ((0, 16), (1, 16))),
        "up_w": normal_values(key_list[7], (D, TRAIN_FF), D ** -0.5, 0.09375, ((0, 16), (1, 16))),
        "cotangent": normal_values(key_list[8], (ROWS, TRAIN_FF), 1.0, 6.0, ((0, 16), (1, 16))),
    }


def reference(candidates, hold_gate, hold_up, probe, chosen, counts, gate_w, up_w, cotangent):
    hold_g = jnp.dot(candidates, hold_gate, preferred_element_type=jnp.float32)
    hold_u = jnp.dot(candidates, hold_up, preferred_element_type=jnp.float32)
    score = jnp.sum(jax.nn.silu(hold_g) * hold_u * probe[None, :], axis=1)
    cand_weight = jax.nn.sigmoid(score)
    flat = chosen.reshape(-1).astype(jnp.int32)
    valid = (jnp.arange(CAP, dtype=jnp.int32)[None, :] < counts[:, None]).reshape(-1)
    row_x = jnp.where(valid[:, None], jnp.take(candidates, flat, axis=0), jnp.zeros((), candidates.dtype)).astype(jnp.bfloat16)
    row_weight = jnp.where(valid, jnp.take(cand_weight, flat), jnp.zeros((), jnp.float32)).astype(jnp.bfloat16)
    gate = jnp.dot(row_x, gate_w, preferred_element_type=jnp.float32)
    up = jnp.dot(row_x, up_w, preferred_element_type=jnp.float32)
    hidden = (jax.nn.silu(gate) * up).astype(jnp.bfloat16)
    back = cotangent.astype(jnp.float32) * row_weight.astype(jnp.float32)[:, None]
    sig = jax.nn.sigmoid(gate)
    d_up = (back * gate * sig).astype(jnp.bfloat16)
    d_gate = (back * up * sig * (1.0 + gate * (1.0 - sig))).astype(jnp.bfloat16)
    grad_gate = jnp.dot(row_x.T, d_gate, preferred_element_type=jnp.float32).astype(jnp.bfloat16)
    grad_up = jnp.dot(row_x.T, d_up, preferred_element_type=jnp.float32).astype(jnp.bfloat16)
    return (grad_gate, grad_up, hidden, cand_weight)
```

```python
import jax
import jax.numpy as jnp
from jax import lax
from jax.sharding import PartitionSpec as P


def gather_by_a2a(x, axis_name, axis):
    parts = lax.psum(1, axis_name)
    stacked = lax.all_to_all(
        jnp.broadcast_to(x[None], (parts,) + x.shape), axis_name, split_axis=0, concat_axis=0, tiled=True
    )
    stacked = jnp.moveaxis(stacked, 0, axis)
    shape = list(x.shape)
    shape[axis] *= parts
    return stacked.reshape(shape)


def on_device(candidates, hold_gate, hold_up, probe, chosen, counts, gate_w, up_w, cotangent):
    cand_dev = candidates.shape[0]
    shards = chosen.shape[0]
    slots = chosen.shape[1]
    full_w = (
        lax.all_gather(gate_w, "dp", axis=0, tiled=True),
        lax.all_gather(up_w, "dp", axis=0, tiled=True),
    )
    own_index = lax.axis_index("dp")
    source = chosen // cand_dev
    local_row = (chosen % cand_dev).reshape(-1)
    usable = ((jnp.arange(slots, dtype=jnp.int32)[None, :] < counts[:, None]) & (source == own_index)).reshape(-1)
    onehot = (
        (local_row[:, None] == jnp.arange(cand_dev, dtype=jnp.int32)[None, :]) & usable[:, None]
    ).astype(jnp.bfloat16)
    picked = jnp.dot(onehot, candidates, preferred_element_type=jnp.float32).astype(jnp.bfloat16)
    picked = picked.reshape(shards, slots, candidates.shape[1])
    arrived = lax.all_to_all(picked, "dp", split_axis=0, concat_axis=0, tiled=True)
    row_slab = jnp.sum(arrived.astype(jnp.float32), axis=0).astype(jnp.bfloat16)
    row_x = gather_by_a2a(row_slab, "mp", 1)
    row_slices = lax.all_to_all(row_x, "dp", split_axis=1, concat_axis=0, tiled=True)

    incoming = lax.all_gather(candidates, "mp", axis=1, tiled=True)
    hold_g = jnp.dot(incoming, hold_gate, preferred_element_type=jnp.float32)
    hold_u = jnp.dot(incoming, hold_up, preferred_element_type=jnp.float32)
    partial_score = jnp.sum(jax.nn.silu(hold_g) * hold_u * probe[None, :], axis=1)
    score = lax.psum(partial_score, "mp")
    cand_weight = jax.nn.sigmoid(score)
    picked_weight = jnp.dot(
        onehot, cand_weight.astype(jnp.bfloat16)[:, None], preferred_element_type=jnp.float32
    ).astype(jnp.bfloat16).reshape(shards, slots)
    arrived_weight = lax.all_to_all(picked_weight, "dp", split_axis=0, concat_axis=0, tiled=True)
    row_weight = jnp.sum(arrived_weight.astype(jnp.float32), axis=0)

    gate = jnp.dot(row_x, full_w[0], preferred_element_type=jnp.float32)
    up = jnp.dot(row_x, full_w[1], preferred_element_type=jnp.float32)
    hidden = (jax.nn.silu(gate) * up).astype(jnp.bfloat16)
    back = cotangent.astype(jnp.float32) * row_weight[:, None]
    sig = jax.nn.sigmoid(gate)
    d_up = (back * gate * sig).astype(jnp.bfloat16)
    d_gate = (back * up * sig * (1.0 + gate * (1.0 - sig))).astype(jnp.bfloat16)
    contract_rows = (((0,), (0,)), ((), ()))
    incoming = (
        lax.all_gather(d_gate, "dp", axis=0, tiled=True),
        lax.all_gather(d_up, "dp", axis=0, tiled=True),
    )
    grad_g = lax.dot_general(
        row_slices, incoming[0], contract_rows, preferred_element_type=jnp.float32
    )
    grad_u = lax.dot_general(
        row_slices, incoming[1], contract_rows, preferred_element_type=jnp.float32
    )
    return (grad_g.astype(jnp.bfloat16), grad_u.astype(jnp.bfloat16), hidden, cand_weight)


def solution(mesh):
    placed = (
        P("dp", "mp"),
        P(None, "mp"),
        P(None, "mp"),
        P("mp"),
        P(),
        P(),
        P("dp", "mp"),
        P("dp", "mp"),
        P("dp", "mp"),
    )
    return jax.shard_map(
        on_device,
        mesh=mesh,
        in_specs=placed,
        out_specs=(P("dp", "mp"), P("dp", "mp"), P("dp", "mp"), P("dp")),
        check_vma=False,
    )
```

```python
import jax
import jax.numpy as jnp
from jax import lax
from jax.sharding import PartitionSpec as P


def gather_by_a2a(x, axis_name, axis):
    parts = lax.psum(1, axis_name)
    stacked = lax.all_to_all(
        jnp.broadcast_to(x[None], (parts,) + x.shape), axis_name, split_axis=0, concat_axis=0, tiled=True
    )
    stacked = jnp.moveaxis(stacked, 0, axis)
    shape = list(x.shape)
    shape[axis] *= parts
    return stacked.reshape(shape)


def gather_rows(x):
    by_z = lax.all_gather(x, "z", axis=0)
    both = lax.all_gather(by_z, "core", axis=1)
    return both.reshape((-1,) + x.shape[1:])


def on_device(candidates, hold_gate, hold_up, probe, chosen, counts, gate_w, up_w, cotangent):
    cand_dev = candidates.shape[0]
    shards = chosen.shape[0]
    slots = chosen.shape[1]
    full_w = (
        gather_rows(gate_w),
        gather_rows(up_w),
    )
    own_index = lax.axis_index("z") * lax.psum(1, "core") + lax.axis_index("core")
    source = chosen // cand_dev
    local_row = (chosen % cand_dev).reshape(-1)
    usable = ((jnp.arange(slots, dtype=jnp.int32)[None, :] < counts[:, None]) & (source == own_index)).reshape(-1)
    onehot = (
        (local_row[:, None] == jnp.arange(cand_dev, dtype=jnp.int32)[None, :]) & usable[:, None]
    ).astype(jnp.bfloat16)
    picked = jnp.dot(onehot, candidates, preferred_element_type=jnp.float32).astype(jnp.bfloat16)
    picked = picked.reshape(shards, slots, candidates.shape[1])
    arrived = lax.all_to_all(picked, DP, split_axis=0, concat_axis=0, tiled=True)
    row_slab = jnp.sum(arrived.astype(jnp.float32), axis=0).astype(jnp.bfloat16)
    row_x = gather_by_a2a(row_slab, "mp", 1)
    row_slices = lax.all_to_all(row_x, DP, split_axis=1, concat_axis=0, tiled=True)

    incoming = gather_by_a2a(candidates, "mp", 1)
    hold_g = jnp.dot(incoming, hold_gate, preferred_element_type=jnp.float32)
    hold_u = jnp.dot(incoming, hold_up, preferred_element_type=jnp.float32)
    partial_score = jnp.sum(jax.nn.silu(hold_g) * hold_u * probe[None, :], axis=1)
    score = lax.psum(partial_score, "mp")
    cand_weight = jax.nn.sigmoid(score)
    picked_weight = jnp.dot(
        onehot, cand_weight.astype(jnp.bfloat16)[:, None], preferred_element_type=jnp.float32
    ).astype(jnp.bfloat16).reshape(shards, slots)
    arrived_weight = lax.all_to_all(picked_weight, DP, split_axis=0, concat_axis=0, tiled=True)
    row_weight = jnp.sum(arrived_weight.astype(jnp.float32), axis=0)

    gate = jnp.dot(row_x, full_w[0], preferred_element_type=jnp.float32)
    up = jnp.dot(row_x, full_w[1], preferred_element_type=jnp.float32)
    hidden = (jax.nn.silu(gate) * up).astype(jnp.bfloat16)
    back = cotangent.astype(jnp.float32) * row_weight[:, None]
    sig = jax.nn.sigmoid(gate)
    d_up = (back * gate * sig).astype(jnp.bfloat16)
    d_gate = (back * up * sig * (1.0 + gate * (1.0 - sig))).astype(jnp.bfloat16)
    contract_rows = (((0,), (0,)), ((), ()))
    incoming = (
        gather_rows(d_gate),
        gather_rows(d_up),
    )
    grad_g = lax.dot_general(
        row_slices, incoming[0], contract_rows, preferred_element_type=jnp.float32
    )
    grad_u = lax.dot_general(
        row_slices, incoming[1], contract_rows, preferred_element_type=jnp.float32
    )
    return (grad_g.astype(jnp.bfloat16), grad_u.astype(jnp.bfloat16), hidden, cand_weight)


DP = ("z", "core")


def solution(mesh):
    cores = 2
    mesh = jax.sharding.Mesh(
        mesh.devices.reshape(mesh.devices.shape[0] // cores, cores, mesh.devices.shape[1]), ("z", "core", "mp")
    )
    placed = (
        P(DP, "mp"),
        P(None, "mp"),
        P(None, "mp"),
        P("mp"),
        P(),
        P(),
        P(DP, "mp"),
        P(DP, "mp"),
        P(DP, "mp"),
    )
    return jax.shard_map(
        on_device,
        mesh=mesh,
        in_specs=placed,
        out_specs=(P(DP, "mp"), P(DP, "mp"), P(DP, "mp"), P(DP)),
        check_vma=False,
    )
```

```python
import jax
import jax.numpy as jnp
from jax import lax
from jax.sharding import PartitionSpec as P


def gather_by_a2a(x, axis_name, axis):
    parts = lax.psum(1, axis_name)
    stacked = lax.all_to_all(
        jnp.broadcast_to(x[None], (parts,) + x.shape), axis_name, split_axis=0, concat_axis=0, tiled=True
    )
    stacked = jnp.moveaxis(stacked, 0, axis)
    shape = list(x.shape)
    shape[axis] *= parts
    return stacked.reshape(shape)


def on_device(candidates, hold_gate, hold_up, probe, chosen, counts, gate_w, up_w, cotangent):
    cand_dev = candidates.shape[0]
    shards = chosen.shape[0]
    slots = chosen.shape[1]
    full_w = (
        lax.all_gather(gate_w, "dp", axis=0, tiled=True),
        lax.all_gather(up_w, "dp", axis=0, tiled=True),
    )
    own_index = lax.axis_index("dp")
    source = chosen // cand_dev
    local_row = (chosen % cand_dev).reshape(-1)
    usable = ((jnp.arange(slots, dtype=jnp.int32)[None, :] < counts[:, None]) & (source == own_index)).reshape(-1)
    onehot = (
        (local_row[:, None] == jnp.arange(cand_dev, dtype=jnp.int32)[None, :]) & usable[:, None]
    ).astype(jnp.bfloat16)
    picked = jnp.dot(onehot, candidates, preferred_element_type=jnp.float32).astype(jnp.bfloat16)
    picked = picked.reshape(shards, slots, candidates.shape[1])
    arrived = lax.all_to_all(picked, "dp", split_axis=0, concat_axis=0, tiled=True)
    row_slab = jnp.sum(arrived.astype(jnp.float32), axis=0).astype(jnp.bfloat16)
    row_x = gather_by_a2a(row_slab, "mp", 1)
    row_slices = lax.all_to_all(row_x, "dp", split_axis=1, concat_axis=0, tiled=True)

    incoming = gather_by_a2a(candidates, "mp", 1)
    hold_g = jnp.dot(incoming, hold_gate, preferred_element_type=jnp.float32)
    hold_u = jnp.dot(incoming, hold_up, preferred_element_type=jnp.float32)
    partial_score = jnp.sum(jax.nn.silu(hold_g) * hold_u * probe[None, :], axis=1)
    score = jnp.sum(gather_by_a2a(partial_score[None, :], "mp", 0), axis=0)
    cand_weight = jax.nn.sigmoid(score)
    picked_weight = jnp.dot(
        onehot, cand_weight.astype(jnp.bfloat16)[:, None], preferred_element_type=jnp.float32
    ).astype(jnp.bfloat16).reshape(shards, slots)
    arrived_weight = lax.all_to_all(picked_weight, "dp", split_axis=0, concat_axis=0, tiled=True)
    row_weight = jnp.sum(arrived_weight.astype(jnp.float32), axis=0)

    gate = jnp.dot(row_x, full_w[0], preferred_element_type=jnp.float32)
    up = jnp.dot(row_x, full_w[1], preferred_element_type=jnp.float32)
    hidden = (jax.nn.silu(gate) * up).astype(jnp.bfloat16)
    back = cotangent.astype(jnp.float32) * row_weight[:, None]
    sig = jax.nn.sigmoid(gate)
    d_up = (back * gate * sig).astype(jnp.bfloat16)
    d_gate = (back * up * sig * (1.0 + gate * (1.0 - sig))).astype(jnp.bfloat16)
    contract_rows = (((0,), (0,)), ((), ()))
    incoming = (
        lax.all_gather(d_gate, "dp", axis=0, tiled=True),
        lax.all_gather(d_up, "dp", axis=0, tiled=True),
    )
    grad_g = lax.dot_general(
        row_slices, incoming[0], contract_rows, preferred_element_type=jnp.float32
    )
    grad_u = lax.dot_general(
        row_slices, incoming[1], contract_rows, preferred_element_type=jnp.float32
    )
    return (grad_g.astype(jnp.bfloat16), grad_u.astype(jnp.bfloat16), hidden, cand_weight)


def solution(mesh):
    placed = (
        P("dp", "mp"),
        P(None, "mp"),
        P(None, "mp"),
        P("mp"),
        P(),
        P(),
        P("dp", "mp"),
        P("dp", "mp"),
        P("dp", "mp"),
    )
    return jax.shard_map(
        on_device,
        mesh=mesh,
        in_specs=placed,
        out_specs=(P("dp", "mp"), P("dp", "mp"), P("dp", "mp"), P("dp")),
        check_vma=False,
    )
```

```python
import jax
import jax.numpy as jnp
from jax import lax
from jax.sharding import PartitionSpec as P


def gather_by_a2a(x, axis_name, axis):
    parts = lax.psum(1, axis_name)
    stacked = lax.all_to_all(
        jnp.broadcast_to(x[None], (parts,) + x.shape), axis_name, split_axis=0, concat_axis=0, tiled=True
    )
    stacked = jnp.moveaxis(stacked, 0, axis)
    shape = list(x.shape)
    shape[axis] *= parts
    return stacked.reshape(shape)


def on_device(candidates, hold_gate, hold_up, probe, chosen, counts, gate_w, up_w, cotangent):
    cand_dev = candidates.shape[0]
    shards = chosen.shape[0]
    slots = chosen.shape[1]
    full_w = (
        lax.all_gather(gate_w, "dp", axis=0, tiled=True),
        lax.all_gather(up_w, "dp", axis=0, tiled=True),
    )
    all_cands = lax.all_gather(candidates, "dp", axis=0, tiled=True)
    own_index = lax.axis_index("dp")
    source = chosen // cand_dev
    local_row = (chosen % cand_dev).reshape(-1)
    valid = jnp.arange(slots, dtype=jnp.int32)[None, :] < counts[:, None]
    usable = (valid & (source == own_index)).reshape(-1)
    onehot = (
        (local_row[:, None] == jnp.arange(cand_dev, dtype=jnp.int32)[None, :]) & usable[:, None]
    ).astype(jnp.bfloat16)
    own_chosen = lax.dynamic_index_in_dim(chosen, own_index, 0, keepdims=False)
    own_valid = lax.dynamic_index_in_dim(valid, own_index, 0, keepdims=False)
    own_onehot = (
        (own_chosen[:, None] == jnp.arange(all_cands.shape[0], dtype=jnp.int32)[None, :]) & own_valid[:, None]
    ).astype(jnp.bfloat16)
    row_slab = jnp.dot(own_onehot, all_cands, preferred_element_type=jnp.float32).astype(jnp.bfloat16)
    row_x = gather_by_a2a(row_slab, "mp", 1)
    row_slices = lax.all_to_all(row_x, "dp", split_axis=1, concat_axis=0, tiled=True)

    incoming = gather_by_a2a(candidates, "mp", 1)
    hold_g = jnp.dot(incoming, hold_gate, preferred_element_type=jnp.float32)
    hold_u = jnp.dot(incoming, hold_up, preferred_element_type=jnp.float32)
    partial_score = jnp.sum(jax.nn.silu(hold_g) * hold_u * probe[None, :], axis=1)
    score = jnp.sum(gather_by_a2a(partial_score[None, :], "mp", 0), axis=0)
    cand_weight = jax.nn.sigmoid(score)
    picked_weight = jnp.dot(
        onehot, cand_weight.astype(jnp.bfloat16)[:, None], preferred_element_type=jnp.float32
    ).astype(jnp.bfloat16).reshape(shards, slots)
    arrived_weight = lax.all_to_all(picked_weight, "dp", split_axis=0, concat_axis=0, tiled=True)
    row_weight = jnp.sum(arrived_weight.astype(jnp.float32), axis=0)

    gate = jnp.dot(row_x, full_w[0], preferred_element_type=jnp.float32)
    up = jnp.dot(row_x, full_w[1], preferred_element_type=jnp.float32)
    hidden = (jax.nn.silu(gate) * up).astype(jnp.bfloat16)
    back = cotangent.astype(jnp.float32) * row_weight[:, None]
    sig = jax.nn.sigmoid(gate)
    d_up = (back * gate * sig).astype(jnp.bfloat16)
    d_gate = (back * up * sig * (1.0 + gate * (1.0 - sig))).astype(jnp.bfloat16)
    contract_rows = (((0,), (0,)), ((), ()))
    incoming = (
        lax.all_gather(d_gate, "dp", axis=0, tiled=True),
        lax.all_gather(d_up, "dp", axis=0, tiled=True),
    )
    grad_g = lax.dot_general(
        row_slices, incoming[0], contract_rows, preferred_element_type=jnp.float32
    )
    grad_u = lax.dot_general(
        row_slices, incoming[1], contract_rows, preferred_element_type=jnp.float32
    )
    return (grad_g.astype(jnp.bfloat16), grad_u.astype(jnp.bfloat16), hidden, cand_weight)


def solution(mesh):
    placed = (
        P("dp", "mp"),
        P(None, "mp"),
        P(None, "mp"),
        P("mp"),
        P(),
        P(),
        P("dp", "mp"),
        P("dp", "mp"),
        P("dp", "mp"),
    )
    return jax.shard_map(
        on_device,
        mesh=mesh,
        in_specs=placed,
        out_specs=(P("dp", "mp"), P("dp", "mp"), P("dp", "mp"), P("dp")),
        check_vma=False,
    )
```

```python
import jax
import jax.numpy as jnp
from jax import lax
from jax.sharding import PartitionSpec as P


def gather_by_a2a(x, axis_name, axis):
    parts = lax.psum(1, axis_name)
    stacked = lax.all_to_all(
        jnp.broadcast_to(x[None], (parts,) + x.shape), axis_name, split_axis=0, concat_axis=0, tiled=True
    )
    stacked = jnp.moveaxis(stacked, 0, axis)
    shape = list(x.shape)
    shape[axis] *= parts
    return stacked.reshape(shape)


def on_device(candidates, hold_gate, hold_up, probe, chosen, counts, gate_w, up_w, cotangent):
    cand_dev = candidates.shape[0]
    shards = chosen.shape[0]
    slots = chosen.shape[1]
    width = candidates.shape[1]
    ff = gate_w.shape[1]
    merged = lax.all_gather(jnp.concatenate([candidates, gate_w, up_w], axis=1), "dp", axis=0, tiled=True)
    all_cands = merged[:, :width]
    full_w = (merged[:, width:width + ff], merged[:, width + ff:])
    own_index = lax.axis_index("dp")
    source = chosen // cand_dev
    local_row = (chosen % cand_dev).reshape(-1)
    valid = jnp.arange(slots, dtype=jnp.int32)[None, :] < counts[:, None]
    usable = (valid & (source == own_index)).reshape(-1)
    onehot = (
        (local_row[:, None] == jnp.arange(cand_dev, dtype=jnp.int32)[None, :]) & usable[:, None]
    ).astype(jnp.bfloat16)
    own_chosen = lax.dynamic_index_in_dim(chosen, own_index, 0, keepdims=False)
    own_valid = lax.dynamic_index_in_dim(valid, own_index, 0, keepdims=False)
    own_onehot = (
        (own_chosen[:, None] == jnp.arange(all_cands.shape[0], dtype=jnp.int32)[None, :]) & own_valid[:, None]
    ).astype(jnp.bfloat16)
    row_slab = jnp.dot(own_onehot, all_cands, preferred_element_type=jnp.float32).astype(jnp.bfloat16)
    row_x = gather_by_a2a(row_slab, "mp", 1)
    parts = lax.psum(1, "dp")
    row_blocks = row_x.reshape(row_x.shape[0], parts, -1).transpose(1, 0, 2)
    row_slices = lax.all_to_all(row_blocks, "dp", split_axis=0, concat_axis=0, tiled=True)
    row_slices = row_slices.reshape(-1, row_blocks.shape[2])

    incoming = gather_by_a2a(candidates, "mp", 1)
    hold_g = jnp.dot(incoming, hold_gate, preferred_element_type=jnp.float32)
    hold_u = jnp.dot(incoming, hold_up, preferred_element_type=jnp.float32)
    partial_score = jnp.sum(jax.nn.silu(hold_g) * hold_u * probe[None, :], axis=1)
    score = jnp.sum(gather_by_a2a(partial_score[None, :], "mp", 0), axis=0)
    cand_weight = jax.nn.sigmoid(score)
    picked_weight = jnp.dot(
        onehot, cand_weight.astype(jnp.bfloat16)[:, None], preferred_element_type=jnp.float32
    ).astype(jnp.bfloat16).reshape(shards, slots)
    arrived_weight = lax.all_to_all(picked_weight, "dp", split_axis=0, concat_axis=0, tiled=True)
    row_weight = jnp.sum(arrived_weight.astype(jnp.float32), axis=0)

    gate = jnp.dot(row_x, full_w[0], preferred_element_type=jnp.float32)
    up = jnp.dot(row_x, full_w[1], preferred_element_type=jnp.float32)
    hidden = (jax.nn.silu(gate) * up).astype(jnp.bfloat16)
    back = cotangent.astype(jnp.float32) * row_weight[:, None]
    sig = jax.nn.sigmoid(gate)
    d_up = (back * gate * sig).astype(jnp.bfloat16)
    d_gate = (back * up * sig * (1.0 + gate * (1.0 - sig))).astype(jnp.bfloat16)
    contract_rows = (((0,), (0,)), ((), ()))
    both_d = lax.all_gather(jnp.concatenate([d_gate, d_up], axis=1), "dp", axis=0, tiled=True)
    incoming = (both_d[:, :ff], both_d[:, ff:])
    grad_g = lax.dot_general(
        row_slices, incoming[0], contract_rows, preferred_element_type=jnp.float32
    )
    grad_u = lax.dot_general(
        row_slices, incoming[1], contract_rows, preferred_element_type=jnp.float32
    )
    return (grad_g.astype(jnp.bfloat16), grad_u.astype(jnp.bfloat16), hidden, cand_weight)


def solution(mesh):
    placed = (
        P("dp", "mp"),
        P(None, "mp"),
        P(None, "mp"),
        P("mp"),
        P(),
        P(),
        P("dp", "mp"),
        P("dp", "mp"),
        P("dp", "mp"),
    )
    return jax.shard_map(
        on_device,
        mesh=mesh,
        in_specs=placed,
        out_specs=(P("dp", "mp"), P("dp", "mp"), P("dp", "mp"), P("dp")),
        check_vma=False,
    )
```

```python
import jax
import jax.numpy as jnp
from jax import lax
from jax.sharding import PartitionSpec as P


def gather_by_a2a(x, axis_name, axis):
    parts = lax.psum(1, axis_name)
    stacked = lax.all_to_all(
        jnp.broadcast_to(x[None], (parts,) + x.shape), axis_name, split_axis=0, concat_axis=0, tiled=True
    )
    stacked = jnp.moveaxis(stacked, 0, axis)
    shape = list(x.shape)
    shape[axis] *= parts
    return stacked.reshape(shape)


def on_device(candidates, hold_gate, hold_up, probe, chosen, counts, gate_w, up_w, cotangent):
    cand_dev = candidates.shape[0]
    shards = chosen.shape[0]
    slots = chosen.shape[1]
    width = candidates.shape[1]
    ff = gate_w.shape[1]
    merged = lax.all_gather(jnp.concatenate([candidates, gate_w, up_w], axis=1), "dp", axis=0, tiled=True)
    all_cands = merged[:, :width]
    full_w = (merged[:, width:width + ff], merged[:, width + ff:])
    own_index = lax.axis_index("dp")
    source = chosen // cand_dev
    local_row = (chosen % cand_dev).reshape(-1)
    valid = jnp.arange(slots, dtype=jnp.int32)[None, :] < counts[:, None]
    usable = (valid & (source == own_index)).reshape(-1)
    onehot = (
        (local_row[:, None] == jnp.arange(cand_dev, dtype=jnp.int32)[None, :]) & usable[:, None]
    ).astype(jnp.bfloat16)
    own_chosen = lax.dynamic_index_in_dim(chosen, own_index, 0, keepdims=False)
    own_valid = lax.dynamic_index_in_dim(valid, own_index, 0, keepdims=False)
    own_onehot = (
        (own_chosen[:, None] == jnp.arange(all_cands.shape[0], dtype=jnp.int32)[None, :]) & own_valid[:, None]
    ).astype(jnp.bfloat16)
    row_slab = jnp.dot(own_onehot, all_cands, preferred_element_type=jnp.float32).astype(jnp.bfloat16)
    row_x = gather_by_a2a(row_slab, "mp", 1)

    incoming = gather_by_a2a(candidates, "mp", 1)
    parts = lax.psum(1, "dp")
    by_feature = incoming.reshape(cand_dev, parts, -1).transpose(1, 0, 2)
    by_feature = lax.all_to_all(by_feature, "dp", split_axis=0, concat_axis=0, tiled=True)
    by_feature = by_feature.reshape(-1, by_feature.shape[2])
    all_onehot = (
        (chosen.reshape(-1)[:, None] == jnp.arange(by_feature.shape[0], dtype=jnp.int32)[None, :])
        & valid.reshape(-1)[:, None]
    ).astype(jnp.bfloat16)
    row_slices = jnp.dot(all_onehot, by_feature, preferred_element_type=jnp.float32).astype(jnp.bfloat16)
    hold_g = jnp.dot(incoming, hold_gate, preferred_element_type=jnp.float32)
    hold_u = jnp.dot(incoming, hold_up, preferred_element_type=jnp.float32)
    partial_score = jnp.sum(jax.nn.silu(hold_g) * hold_u * probe[None, :], axis=1)
    score = jnp.sum(gather_by_a2a(partial_score[None, :], "mp", 0), axis=0)
    cand_weight = jax.nn.sigmoid(score)
    picked_weight = jnp.dot(
        onehot, cand_weight.astype(jnp.bfloat16)[:, None], preferred_element_type=jnp.float32
    ).astype(jnp.bfloat16).reshape(shards, slots)
    arrived_weight = lax.all_to_all(picked_weight, "dp", split_axis=0, concat_axis=0, tiled=True)
    row_weight = jnp.sum(arrived_weight.astype(jnp.float32), axis=0)

    row_x, row_slices = lax.optimization_barrier((row_x, row_slices))
    gate = jnp.dot(row_x, full_w[0], preferred_element_type=jnp.float32)
    up = jnp.dot(row_x, full_w[1], preferred_element_type=jnp.float32)
    hidden = (jax.nn.silu(gate) * up).astype(jnp.bfloat16)
    back = cotangent.astype(jnp.float32) * row_weight[:, None]
    sig = jax.nn.sigmoid(gate)
    d_up = (back * gate * sig).astype(jnp.bfloat16)
    d_gate = (back * up * sig * (1.0 + gate * (1.0 - sig))).astype(jnp.bfloat16)
    contract_rows = (((0,), (0,)), ((), ()))
    both_d = lax.all_gather(jnp.concatenate([d_gate, d_up], axis=1), "dp", axis=0, tiled=True)
    incoming = (both_d[:, :ff], both_d[:, ff:])
    grad_g = lax.dot_general(
        row_slices, incoming[0], contract_rows, preferred_element_type=jnp.float32
    )
    grad_u = lax.dot_general(
        row_slices, incoming[1], contract_rows, preferred_element_type=jnp.float32
    )
    return (grad_g.astype(jnp.bfloat16), grad_u.astype(jnp.bfloat16), hidden, cand_weight)


def solution(mesh):
    placed = (
        P("dp", "mp"),
        P(None, "mp"),
        P(None, "mp"),
        P("mp"),
        P(),
        P(),
        P("dp", "mp"),
        P("dp", "mp"),
        P("dp", "mp"),
    )
    return jax.shard_map(
        on_device,
        mesh=mesh,
        in_specs=placed,
        out_specs=(P("dp", "mp"), P("dp", "mp"), P("dp", "mp"), P("dp")),
        check_vma=False,
    )
```

```python
import jax
import jax.numpy as jnp
from jax import lax
from jax.sharding import PartitionSpec as P


def gather_by_a2a(x, axis_name, axis):
    parts = lax.psum(1, axis_name)
    stacked = lax.all_to_all(
        jnp.broadcast_to(x[None], (parts,) + x.shape), axis_name, split_axis=0, concat_axis=0, tiled=True
    )
    stacked = jnp.moveaxis(stacked, 0, axis)
    shape = list(x.shape)
    shape[axis] *= parts
    return stacked.reshape(shape)


def on_device(candidates, hold_gate, hold_up, probe, chosen, counts, gate_w, up_w, cotangent):
    cand_dev = candidates.shape[0]
    shards = chosen.shape[0]
    slots = chosen.shape[1]
    width = candidates.shape[1]
    ff = gate_w.shape[1]
    merged = lax.all_gather(jnp.concatenate([candidates, gate_w], axis=1), "dp", axis=0, tiled=True)
    all_cands = merged[:, :width]
    full_w = (merged[:, width:], lax.all_gather(up_w, "dp", axis=0, tiled=True))
    own_index = lax.axis_index("dp")
    source = chosen // cand_dev
    local_row = (chosen % cand_dev).reshape(-1)
    valid = jnp.arange(slots, dtype=jnp.int32)[None, :] < counts[:, None]
    usable = (valid & (source == own_index)).reshape(-1)
    onehot = (
        (local_row[:, None] == jnp.arange(cand_dev, dtype=jnp.int32)[None, :]) & usable[:, None]
    ).astype(jnp.bfloat16)
    own_chosen = lax.dynamic_index_in_dim(chosen, own_index, 0, keepdims=False)
    own_valid = lax.dynamic_index_in_dim(valid, own_index, 0, keepdims=False)
    own_onehot = (
        (own_chosen[:, None] == jnp.arange(all_cands.shape[0], dtype=jnp.int32)[None, :]) & own_valid[:, None]
    ).astype(jnp.bfloat16)
    row_slab = jnp.dot(own_onehot, all_cands, preferred_element_type=jnp.float32).astype(jnp.bfloat16)
    row_x = gather_by_a2a(row_slab, "mp", 1)
    parts = lax.psum(1, "dp")
    row_blocks = row_x.reshape(row_x.shape[0], parts, -1).transpose(1, 0, 2)
    row_slices = lax.all_to_all(row_blocks, "dp", split_axis=0, concat_axis=0, tiled=True)
    row_slices = row_slices.reshape(-1, row_blocks.shape[2])

    incoming = gather_by_a2a(candidates, "mp", 1)
    hold_g = jnp.dot(incoming, hold_gate, preferred_element_type=jnp.float32)
    hold_u = jnp.dot(incoming, hold_up, preferred_element_type=jnp.float32)
    partial_score = jnp.sum(jax.nn.silu(hold_g) * hold_u * probe[None, :], axis=1)
    score = jnp.sum(gather_by_a2a(partial_score[None, :], "mp", 0), axis=0)
    cand_weight = jax.nn.sigmoid(score)
    picked_weight = jnp.dot(
        onehot, cand_weight.astype(jnp.bfloat16)[:, None], preferred_element_type=jnp.float32
    ).astype(jnp.bfloat16).reshape(shards, slots)
    arrived_weight = lax.all_to_all(picked_weight, "dp", split_axis=0, concat_axis=0, tiled=True)
    row_weight = jnp.sum(arrived_weight.astype(jnp.float32), axis=0)

    gate = jnp.dot(row_x, full_w[0], preferred_element_type=jnp.float32)
    up = jnp.dot(row_x, full_w[1], preferred_element_type=jnp.float32)
    hidden = (jax.nn.silu(gate) * up).astype(jnp.bfloat16)
    back = cotangent.astype(jnp.float32) * row_weight[:, None]
    sig = jax.nn.sigmoid(gate)
    d_up = (back * gate * sig).astype(jnp.bfloat16)
    d_gate = (back * up * sig * (1.0 + gate * (1.0 - sig))).astype(jnp.bfloat16)
    contract_rows = (((0,), (0,)), ((), ()))
    both_d = lax.all_gather(jnp.concatenate([d_gate, d_up], axis=1), "dp", axis=0, tiled=True)
    incoming = (both_d[:, :ff], both_d[:, ff:])
    grad_g = lax.dot_general(
        row_slices, incoming[0], contract_rows, preferred_element_type=jnp.float32
    )
    grad_u = lax.dot_general(
        row_slices, incoming[1], contract_rows, preferred_element_type=jnp.float32
    )
    return (grad_g.astype(jnp.bfloat16), grad_u.astype(jnp.bfloat16), hidden, cand_weight)


def solution(mesh):
    placed = (
        P("dp", "mp"),
        P(None, "mp"),
        P(None, "mp"),
        P("mp"),
        P(),
        P(),
        P("dp", "mp"),
        P("dp", "mp"),
        P("dp", "mp"),
    )
    return jax.shard_map(
        on_device,
        mesh=mesh,
        in_specs=placed,
        out_specs=(P("dp", "mp"), P("dp", "mp"), P("dp", "mp"), P("dp")),
        check_vma=False,
    )
```

```python
import jax
import jax.numpy as jnp
from jax import lax
from jax.sharding import PartitionSpec as P


def gather_by_a2a(x, axis_name, axis):
    parts = lax.psum(1, axis_name)
    stacked = lax.all_to_all(
        jnp.broadcast_to(x[None], (parts,) + x.shape), axis_name, split_axis=0, concat_axis=0, tiled=True
    )
    stacked = jnp.moveaxis(stacked, 0, axis)
    shape = list(x.shape)
    shape[axis] *= parts
    return stacked.reshape(shape)


def ring_gather_rows(x):
    nz = lax.psum(1, "z")
    fwd = [x]
    buf = x
    for _ in range(nz // 2):
        buf = lax.ppermute(buf, "z", [(i, (i + 1) % nz) for i in range(nz)])
        fwd.append(buf)
    bwd = []
    buf = x
    for _ in range(nz - 1 - nz // 2):
        buf = lax.ppermute(buf, "z", [(i, (i - 1) % nz) for i in range(nz)])
        bwd.append(buf)
    rel = jnp.stack([x] + bwd + [fwd[nz - j] for j in range(len(bwd) + 1, nz)], axis=0)
    by_z = jnp.roll(rel, lax.axis_index("z"), axis=0)
    other = lax.ppermute(by_z, "core", [(0, 1), (1, 0)])
    both = jnp.roll(jnp.stack([by_z, other], axis=1), lax.axis_index("core"), axis=1)
    return both.reshape((-1,) + x.shape[1:])


def on_device(candidates, hold_gate, hold_up, probe, chosen, counts, gate_w, up_w, cotangent):
    cand_dev = candidates.shape[0]
    shards = chosen.shape[0]
    slots = chosen.shape[1]
    width = candidates.shape[1]
    ff = gate_w.shape[1]
    all_cands = lax.all_gather(candidates, DP, axis=0, tiled=True)
    full_w = (ring_gather_rows(gate_w), ring_gather_rows(up_w))
    own_index = lax.axis_index("z") * lax.psum(1, "core") + lax.axis_index("core")
    source = chosen // cand_dev
    local_row = (chosen % cand_dev).reshape(-1)
    valid = jnp.arange(slots, dtype=jnp.int32)[None, :] < counts[:, None]
    usable = (valid & (source == own_index)).reshape(-1)
    onehot = (
        (local_row[:, None] == jnp.arange(cand_dev, dtype=jnp.int32)[None, :]) & usable[:, None]
    ).astype(jnp.bfloat16)
    own_chosen = lax.dynamic_index_in_dim(chosen, own_index, 0, keepdims=False)
    own_valid = lax.dynamic_index_in_dim(valid, own_index, 0, keepdims=False)
    own_onehot = (
        (own_chosen[:, None] == jnp.arange(all_cands.shape[0], dtype=jnp.int32)[None, :]) & own_valid[:, None]
    ).astype(jnp.bfloat16)
    row_slab = jnp.dot(own_onehot, all_cands, preferred_element_type=jnp.float32).astype(jnp.bfloat16)
    row_x = gather_by_a2a(row_slab, "mp", 1)
    parts = lax.psum(1, DP)
    row_blocks = row_x.reshape(row_x.shape[0], parts, -1).transpose(1, 0, 2)
    row_slices = lax.all_to_all(row_blocks, DP, split_axis=0, concat_axis=0, tiled=True)
    row_slices = row_slices.reshape(-1, row_blocks.shape[2])

    incoming = gather_by_a2a(candidates, "mp", 1)
    hold_g = jnp.dot(incoming, hold_gate, preferred_element_type=jnp.float32)
    hold_u = jnp.dot(incoming, hold_up, preferred_element_type=jnp.float32)
    partial_score = jnp.sum(jax.nn.silu(hold_g) * hold_u * probe[None, :], axis=1)
    score = jnp.sum(gather_by_a2a(partial_score[None, :], "mp", 0), axis=0)
    cand_weight = jax.nn.sigmoid(score)
    picked_weight = jnp.dot(
        onehot, cand_weight.astype(jnp.bfloat16)[:, None], preferred_element_type=jnp.float32
    ).astype(jnp.bfloat16).reshape(shards, slots)
    arrived_weight = lax.all_to_all(picked_weight, DP, split_axis=0, concat_axis=0, tiled=True)
    row_weight = jnp.sum(arrived_weight.astype(jnp.float32), axis=0)

    gate = jnp.dot(row_x, full_w[0], preferred_element_type=jnp.float32)
    up = jnp.dot(row_x, full_w[1], preferred_element_type=jnp.float32)
    hidden = (jax.nn.silu(gate) * up).astype(jnp.bfloat16)
    back = cotangent.astype(jnp.float32) * row_weight[:, None]
    sig = jax.nn.sigmoid(gate)
    d_up = (back * gate * sig).astype(jnp.bfloat16)
    d_gate = (back * up * sig * (1.0 + gate * (1.0 - sig))).astype(jnp.bfloat16)
    contract_rows = (((0,), (0,)), ((), ()))
    both_d = ring_gather_rows(jnp.concatenate([d_gate, d_up], axis=1))
    incoming = (both_d[:, :ff], both_d[:, ff:])
    grad_g = lax.dot_general(
        row_slices, incoming[0], contract_rows, preferred_element_type=jnp.float32
    )
    grad_u = lax.dot_general(
        row_slices, incoming[1], contract_rows, preferred_element_type=jnp.float32
    )
    return (grad_g.astype(jnp.bfloat16), grad_u.astype(jnp.bfloat16), hidden, cand_weight)


DP = ("z", "core")


def solution(mesh):
    cores = 2
    mesh = jax.sharding.Mesh(
        mesh.devices.reshape(mesh.devices.shape[0] // cores, cores, mesh.devices.shape[1]), ("z", "core", "mp")
    )
    placed = (
        P(DP, "mp"),
        P(None, "mp"),
        P(None, "mp"),
        P("mp"),
        P(),
        P(),
        P(DP, "mp"),
        P(DP, "mp"),
        P(DP, "mp"),
    )
    return jax.shard_map(
        on_device,
        mesh=mesh,
        in_specs=placed,
        out_specs=(P(DP, "mp"), P(DP, "mp"), P(DP, "mp"), P(DP)),
        check_vma=False,
    )
```

```python
import jax
import jax.numpy as jnp
from jax import lax
from jax.sharding import PartitionSpec as P


def gather_by_a2a(x, axis_name, axis):
    parts = lax.psum(1, axis_name)
    stacked = lax.all_to_all(
        jnp.broadcast_to(x[None], (parts,) + x.shape), axis_name, split_axis=0, concat_axis=0, tiled=True
    )
    stacked = jnp.moveaxis(stacked, 0, axis)
    shape = list(x.shape)
    shape[axis] *= parts
    return stacked.reshape(shape)


def ring_gather_rows(x):
    nz = lax.psum(1, "z")
    fwd = [x]
    buf = x
    for _ in range(nz // 2):
        buf = lax.ppermute(buf, "z", [(i, (i + 1) % nz) for i in range(nz)])
        fwd.append(buf)
    bwd = []
    buf = x
    for _ in range(nz - 1 - nz // 2):
        buf = lax.ppermute(buf, "z", [(i, (i - 1) % nz) for i in range(nz)])
        bwd.append(buf)
    rel = jnp.stack([x] + bwd + [fwd[nz - j] for j in range(len(bwd) + 1, nz)], axis=0)
    by_z = jnp.roll(rel, lax.axis_index("z"), axis=0)
    other = lax.ppermute(by_z, "core", [(0, 1), (1, 0)])
    both = jnp.roll(jnp.stack([by_z, other], axis=1), lax.axis_index("core"), axis=1)
    return both.reshape((-1,) + x.shape[1:])


def on_device(candidates, hold_gate, hold_up, probe, chosen, counts, gate_w, up_w, cotangent):
    cand_dev = candidates.shape[0]
    shards = chosen.shape[0]
    slots = chosen.shape[1]
    width = candidates.shape[1]
    ff = gate_w.shape[1]
    merged = lax.all_gather(jnp.concatenate([candidates, gate_w], axis=1), DP, axis=0, tiled=True)
    all_cands = merged[:, :width]
    full_w = (merged[:, width:], ring_gather_rows(up_w))
    own_index = lax.axis_index("z") * lax.psum(1, "core") + lax.axis_index("core")
    source = chosen // cand_dev
    local_row = (chosen % cand_dev).reshape(-1)
    valid = jnp.arange(slots, dtype=jnp.int32)[None, :] < counts[:, None]
    usable = (valid & (source == own_index)).reshape(-1)
    onehot = (
        (local_row[:, None] == jnp.arange(cand_dev, dtype=jnp.int32)[None, :]) & usable[:, None]
    ).astype(jnp.bfloat16)
    own_chosen = lax.dynamic_index_in_dim(chosen, own_index, 0, keepdims=False)
    own_valid = lax.dynamic_index_in_dim(valid, own_index, 0, keepdims=False)
    own_onehot = (
        (own_chosen[:, None] == jnp.arange(all_cands.shape[0], dtype=jnp.int32)[None, :]) & own_valid[:, None]
    ).astype(jnp.bfloat16)
    row_slab = jnp.dot(own_onehot, all_cands, preferred_element_type=jnp.float32).astype(jnp.bfloat16)
    row_x = gather_by_a2a(row_slab, "mp", 1)
    parts = lax.psum(1, DP)
    row_blocks = row_x.reshape(row_x.shape[0], parts, -1).transpose(1, 0, 2)
    row_slices = lax.all_to_all(row_blocks, DP, split_axis=0, concat_axis=0, tiled=True)
    row_slices = row_slices.reshape(-1, row_blocks.shape[2])

    incoming = gather_by_a2a(candidates, "mp", 1)
    hold_g = jnp.dot(incoming, hold_gate, preferred_element_type=jnp.float32)
    hold_u = jnp.dot(incoming, hold_up, preferred_element_type=jnp.float32)
    partial_score = jnp.sum(jax.nn.silu(hold_g) * hold_u * probe[None, :], axis=1)
    score = jnp.sum(gather_by_a2a(partial_score[None, :], "mp", 0), axis=0)
    cand_weight = jax.nn.sigmoid(score)
    picked_weight = jnp.dot(
        onehot, cand_weight.astype(jnp.bfloat16)[:, None], preferred_element_type=jnp.float32
    ).astype(jnp.bfloat16).reshape(shards, slots)
    arrived_weight = lax.all_to_all(picked_weight, DP, split_axis=0, concat_axis=0, tiled=True)
    row_weight = jnp.sum(arrived_weight.astype(jnp.float32), axis=0)

    gate = jnp.dot(row_x, full_w[0], preferred_element_type=jnp.float32)
    up = jnp.dot(row_x, full_w[1], preferred_element_type=jnp.float32)
    hidden = (jax.nn.silu(gate) * up).astype(jnp.bfloat16)
    back = cotangent.astype(jnp.float32) * row_weight[:, None]
    sig = jax.nn.sigmoid(gate)
    d_up = (back * gate * sig).astype(jnp.bfloat16)
    d_gate = (back * up * sig * (1.0 + gate * (1.0 - sig))).astype(jnp.bfloat16)
    contract_rows = (((0,), (0,)), ((), ()))
    both_d = lax.all_gather(jnp.concatenate([d_gate, d_up], axis=1), DP, axis=0, tiled=True)
    incoming = (both_d[:, :ff], both_d[:, ff:])
    grad_g = lax.dot_general(
        row_slices, incoming[0], contract_rows, preferred_element_type=jnp.float32
    )
    grad_u = lax.dot_general(
        row_slices, incoming[1], contract_rows, preferred_element_type=jnp.float32
    )
    return (grad_g.astype(jnp.bfloat16), grad_u.astype(jnp.bfloat16), hidden, cand_weight)


DP = ("z", "core")


def solution(mesh):
    cores = 2
    mesh = jax.sharding.Mesh(
        mesh.devices.reshape(mesh.devices.shape[0] // cores, cores, mesh.devices.shape[1]), ("z", "core", "mp")
    )
    placed = (
        P(DP, "mp"),
        P(None, "mp"),
        P(None, "mp"),
        P("mp"),
        P(),
        P(),
        P(DP, "mp"),
        P(DP, "mp"),
        P(DP, "mp"),
    )
    return jax.shard_map(
        on_device,
        mesh=mesh,
        in_specs=placed,
        out_specs=(P(DP, "mp"), P(DP, "mp"), P(DP, "mp"), P(DP)),
        check_vma=False,
    )
```

```python
import jax
import jax.numpy as jnp
from jax import lax
from jax.sharding import PartitionSpec as P


def gather_by_a2a(x, axis_name, axis):
    parts = lax.psum(1, axis_name)
    stacked = lax.all_to_all(
        jnp.broadcast_to(x[None], (parts,) + x.shape), axis_name, split_axis=0, concat_axis=0, tiled=True
    )
    stacked = jnp.moveaxis(stacked, 0, axis)
    shape = list(x.shape)
    shape[axis] *= parts
    return stacked.reshape(shape)


def on_device(candidates, hold_gate, hold_up, probe, chosen, counts, gate_w, up_w, cotangent):
    cand_dev = candidates.shape[0]
    shards = chosen.shape[0]
    slots = chosen.shape[1]
    width = candidates.shape[1]
    ff = gate_w.shape[1]
    merged = lax.all_gather(jnp.concatenate([candidates, gate_w], axis=1), "dp", axis=0, tiled=True)
    all_cands = merged[:, :width]
    full_w = (merged[:, width:], lax.all_gather(up_w, "dp", axis=0, tiled=True))
    own_index = lax.axis_index("dp")
    source = chosen // cand_dev
    local_row = (chosen % cand_dev).reshape(-1)
    valid = jnp.arange(slots, dtype=jnp.int32)[None, :] < counts[:, None]
    usable = (valid & (source == own_index)).reshape(-1)
    onehot = (
        (local_row[:, None] == jnp.arange(cand_dev, dtype=jnp.int32)[None, :]) & usable[:, None]
    ).astype(jnp.bfloat16)
    own_chosen = lax.dynamic_index_in_dim(chosen, own_index, 0, keepdims=False)
    own_valid = lax.dynamic_index_in_dim(valid, own_index, 0, keepdims=False)
    own_onehot = (
        (own_chosen[:, None] == jnp.arange(all_cands.shape[0], dtype=jnp.int32)[None, :]) & own_valid[:, None]
    ).astype(jnp.bfloat16)
    row_slab = jnp.dot(own_onehot, all_cands, preferred_element_type=jnp.float32).astype(jnp.bfloat16)
    row_x = gather_by_a2a(row_slab, "mp", 1)
    parts = lax.psum(1, "dp")
    row_blocks = row_x.reshape(row_x.shape[0], parts, -1).transpose(1, 0, 2)
    row_slices = lax.all_to_all(row_blocks, "dp", split_axis=0, concat_axis=0, tiled=True)
    row_slices = row_slices.reshape(-1, row_blocks.shape[2])

    incoming = gather_by_a2a(candidates, "mp", 1)
    hold_g = jnp.dot(incoming, hold_gate, preferred_element_type=jnp.float32)
    hold_u = jnp.dot(incoming, hold_up, preferred_element_type=jnp.float32)
    partial_score = jnp.sum(jax.nn.silu(hold_g) * hold_u * probe[None, :], axis=1)
    score = jnp.sum(gather_by_a2a(partial_score[None, :], "mp", 0), axis=0)
    cand_weight = jax.nn.sigmoid(score)
    late_weight, row_x = lax.optimization_barrier((cand_weight, row_x))
    picked_weight = jnp.dot(
        onehot, late_weight.astype(jnp.bfloat16)[:, None], preferred_element_type=jnp.float32
    ).astype(jnp.bfloat16).reshape(shards, slots)
    arrived_weight = lax.all_to_all(picked_weight, "dp", split_axis=0, concat_axis=0, tiled=True)
    row_weight = jnp.sum(arrived_weight.astype(jnp.float32), axis=0)

    gate = jnp.dot(row_x, full_w[0], preferred_element_type=jnp.float32)
    row_slices, up_w_full = lax.optimization_barrier((row_slices, full_w[1]))
    up = jnp.dot(row_x, up_w_full, preferred_element_type=jnp.float32)
    hidden = (jax.nn.silu(gate) * up).astype(jnp.bfloat16)
    back = cotangent.astype(jnp.float32) * row_weight[:, None]
    sig = jax.nn.sigmoid(gate)
    d_up = (back * gate * sig).astype(jnp.bfloat16)
    d_gate = (back * up * sig * (1.0 + gate * (1.0 - sig))).astype(jnp.bfloat16)
    contract_rows = (((0,), (0,)), ((), ()))
    both_d = lax.all_gather(jnp.concatenate([d_gate, d_up], axis=1), "dp", axis=0, tiled=True)
    incoming = (both_d[:, :ff], both_d[:, ff:])
    grad_g = lax.dot_general(
        row_slices, incoming[0], contract_rows, preferred_element_type=jnp.float32
    )
    grad_u = lax.dot_general(
        row_slices, incoming[1], contract_rows, preferred_element_type=jnp.float32
    )
    return (grad_g.astype(jnp.bfloat16), grad_u.astype(jnp.bfloat16), hidden, cand_weight)


def solution(mesh):
    placed = (
        P("dp", "mp"),
        P(None, "mp"),
        P(None, "mp"),
        P("mp"),
        P(),
        P(),
        P("dp", "mp"),
        P("dp", "mp"),
        P("dp", "mp"),
    )
    return jax.shard_map(
        on_device,
        mesh=mesh,
        in_specs=placed,
        out_specs=(P("dp", "mp"), P("dp", "mp"), P("dp", "mp"), P("dp")),
        check_vma=False,
    )
```

```python
import jax
import jax.numpy as jnp
from jax import lax
from jax.sharding import PartitionSpec as P


def gather_by_a2a(x, axis_name, axis):
    parts = lax.psum(1, axis_name)
    stacked = lax.all_to_all(
        jnp.broadcast_to(x[None], (parts,) + x.shape), axis_name, split_axis=0, concat_axis=0, tiled=True
    )
    stacked = jnp.moveaxis(stacked, 0, axis)
    shape = list(x.shape)
    shape[axis] *= parts
    return stacked.reshape(shape)


def on_device(candidates, hold_gate, hold_up, probe, chosen, counts, gate_w, up_w, cotangent):
    cand_dev = candidates.shape[0]
    shards = chosen.shape[0]
    slots = chosen.shape[1]
    width = candidates.shape[1]
    ff = gate_w.shape[1]
    merged = lax.all_gather(jnp.concatenate([candidates, gate_w], axis=1), "dp", axis=0, tiled=True)
    all_cands = merged[:, :width]
    full_w = (merged[:, width:], lax.all_gather(up_w, "dp", axis=0, tiled=True))
    own_index = lax.axis_index("dp")
    source = chosen // cand_dev
    local_row = (chosen % cand_dev).reshape(-1)
    valid = jnp.arange(slots, dtype=jnp.int32)[None, :] < counts[:, None]
    usable = (valid & (source == own_index)).reshape(-1)
    onehot = (
        (local_row[:, None] == jnp.arange(cand_dev, dtype=jnp.int32)[None, :]) & usable[:, None]
    ).astype(jnp.bfloat16)
    own_chosen = lax.dynamic_index_in_dim(chosen, own_index, 0, keepdims=False)
    own_valid = lax.dynamic_index_in_dim(valid, own_index, 0, keepdims=False)
    own_onehot = (
        (own_chosen[:, None] == jnp.arange(all_cands.shape[0], dtype=jnp.int32)[None, :]) & own_valid[:, None]
    ).astype(jnp.bfloat16)
    row_slab = jnp.dot(own_onehot, all_cands, preferred_element_type=jnp.float32).astype(jnp.bfloat16)
    row_x = gather_by_a2a(row_slab, "mp", 1)
    parts = lax.psum(1, "dp")
    row_blocks = row_x.reshape(row_x.shape[0], parts, -1).transpose(1, 0, 2)
    row_slices = lax.all_to_all(row_blocks, "dp", split_axis=0, concat_axis=0, tiled=True)
    row_slices = row_slices.reshape(-1, row_blocks.shape[2])

    incoming = gather_by_a2a(candidates, "mp", 1)
    hold_g = jnp.dot(incoming, hold_gate, preferred_element_type=jnp.float32)
    hold_u = jnp.dot(incoming, hold_up, preferred_element_type=jnp.float32)
    partial_score = jnp.sum(jax.nn.silu(hold_g) * hold_u * probe[None, :], axis=1)
    score = jnp.sum(gather_by_a2a(partial_score[None, :], "mp", 0), axis=0)
    cand_weight = jax.nn.sigmoid(score)
    picked_weight = jnp.dot(
        onehot, cand_weight.astype(jnp.bfloat16)[:, None], preferred_element_type=jnp.float32
    ).astype(jnp.bfloat16).reshape(shards, slots)
    arrived_weight = lax.all_to_all(picked_weight, "dp", split_axis=0, concat_axis=0, tiled=True)
    row_weight = jnp.sum(arrived_weight.astype(jnp.float32), axis=0)

    gate = jnp.dot(row_x, full_w[0], preferred_element_type=jnp.float32)
    up = jnp.dot(row_x, full_w[1], preferred_element_type=jnp.float32)
    hidden = (jax.nn.silu(gate) * up).astype(jnp.bfloat16)
    back = cotangent.astype(jnp.float32) * row_weight[:, None]
    sig = jax.nn.sigmoid(gate)
    d_up = (back * gate * sig).astype(jnp.bfloat16)
    d_gate = (back * up * sig * (1.0 + gate * (1.0 - sig))).astype(jnp.bfloat16)
    contract_rows = (((0,), (0,)), ((), ()))
    d_both, row_slices = lax.optimization_barrier((jnp.concatenate([d_gate, d_up], axis=1), row_slices))
    both_d = lax.all_gather(d_both, "dp", axis=0, tiled=True)
    incoming = (both_d[:, :ff], both_d[:, ff:])
    grad_g = lax.dot_general(
        row_slices, incoming[0], contract_rows, preferred_element_type=jnp.float32
    )
    grad_u = lax.dot_general(
        row_slices, incoming[1], contract_rows, preferred_element_type=jnp.float32
    )
    return (grad_g.astype(jnp.bfloat16), grad_u.astype(jnp.bfloat16), hidden, cand_weight)


def solution(mesh):
    placed = (
        P("dp", "mp"),
        P(None, "mp"),
        P(None, "mp"),
        P("mp"),
        P(),
        P(),
        P("dp", "mp"),
        P("dp", "mp"),
        P("dp", "mp"),
    )
    return jax.shard_map(
        on_device,
        mesh=mesh,
        in_specs=placed,
        out_specs=(P("dp", "mp"), P("dp", "mp"), P("dp", "mp"), P("dp")),
        check_vma=False,
    )
```

```python
import jax
import jax.numpy as jnp
from jax import lax
from jax.sharding import PartitionSpec as P


def gather_by_a2a(x, axis_name, axis):
    parts = lax.psum(1, axis_name)
    stacked = lax.all_to_all(
        jnp.broadcast_to(x[None], (parts,) + x.shape), axis_name, split_axis=0, concat_axis=0, tiled=True
    )
    stacked = jnp.moveaxis(stacked, 0, axis)
    shape = list(x.shape)
    shape[axis] *= parts
    return stacked.reshape(shape)


def on_device(candidates, hold_gate, hold_up, probe, chosen, counts, gate_w, up_w, cotangent):
    cand_dev = candidates.shape[0]
    shards = chosen.shape[0]
    slots = chosen.shape[1]
    width = candidates.shape[1]
    ff = gate_w.shape[1]
    merged = lax.all_gather(jnp.concatenate([candidates, gate_w], axis=1), "dp", axis=0, tiled=True)
    all_cands = merged[:, :width]
    full_w = (merged[:, width:], lax.all_gather(up_w, "dp", axis=0, tiled=True))
    own_index = lax.axis_index("dp")
    source = chosen // cand_dev
    local_row = (chosen % cand_dev).reshape(-1)
    valid = jnp.arange(slots, dtype=jnp.int32)[None, :] < counts[:, None]
    usable = (valid & (source == own_index)).reshape(-1)
    onehot = (
        (local_row[:, None] == jnp.arange(cand_dev, dtype=jnp.int32)[None, :]) & usable[:, None]
    ).astype(jnp.bfloat16)
    own_chosen = lax.dynamic_index_in_dim(chosen, own_index, 0, keepdims=False)
    own_valid = lax.dynamic_index_in_dim(valid, own_index, 0, keepdims=False)
    own_onehot = (
        (own_chosen[:, None] == jnp.arange(all_cands.shape[0], dtype=jnp.int32)[None, :]) & own_valid[:, None]
    ).astype(jnp.bfloat16)
    row_slab = jnp.dot(own_onehot, all_cands, preferred_element_type=jnp.float32).astype(jnp.bfloat16)
    row_x = gather_by_a2a(row_slab, "mp", 1)
    dp_size = lax.psum(1, "dp")
    mp_size = lax.psum(1, "mp")
    all_onehot = (
        (chosen.reshape(-1)[:, None] == jnp.arange(all_cands.shape[0], dtype=jnp.int32)[None, :])
        & valid.reshape(-1)[:, None]
    ).astype(jnp.bfloat16)
    own_slices = jnp.dot(all_onehot, all_cands, preferred_element_type=jnp.float32).astype(jnp.bfloat16)
    swap = [
        (a * mp_size + b, b * mp_size + a) for a in range(dp_size) for b in range(mp_size) if a != b
    ]
    swapped = lax.ppermute(own_slices, ("dp", "mp"), swap)
    row_slices = jnp.where(own_index == lax.axis_index("mp"), own_slices, swapped)

    incoming = gather_by_a2a(candidates, "mp", 1)
    hold_g = jnp.dot(incoming, hold_gate, preferred_element_type=jnp.float32)
    hold_u = jnp.dot(incoming, hold_up, preferred_element_type=jnp.float32)
    partial_score = jnp.sum(jax.nn.silu(hold_g) * hold_u * probe[None, :], axis=1)
    score = jnp.sum(gather_by_a2a(partial_score[None, :], "mp", 0), axis=0)
    cand_weight = jax.nn.sigmoid(score)
    picked_weight = jnp.dot(
        onehot, cand_weight.astype(jnp.bfloat16)[:, None], preferred_element_type=jnp.float32
    ).astype(jnp.bfloat16).reshape(shards, slots)
    arrived_weight = lax.all_to_all(picked_weight, "dp", split_axis=0, concat_axis=0, tiled=True)
    row_weight = jnp.sum(arrived_weight.astype(jnp.float32), axis=0)

    gate = jnp.dot(row_x, full_w[0], preferred_element_type=jnp.float32)
    up = jnp.dot(row_x, full_w[1], preferred_element_type=jnp.float32)
    hidden = (jax.nn.silu(gate) * up).astype(jnp.bfloat16)
    back = cotangent.astype(jnp.float32) * row_weight[:, None]
    sig = jax.nn.sigmoid(gate)
    d_up = (back * gate * sig).astype(jnp.bfloat16)
    d_gate = (back * up * sig * (1.0 + gate * (1.0 - sig))).astype(jnp.bfloat16)
    contract_rows = (((0,), (0,)), ((), ()))
    d_both, row_slices = lax.optimization_barrier((jnp.concatenate([d_gate, d_up], axis=1), row_slices))
    both_d = lax.all_gather(d_both, "dp", axis=0, tiled=True)
    incoming = (both_d[:, :ff], both_d[:, ff:])
    grad_g = lax.dot_general(
        row_slices, incoming[0], contract_rows, preferred_element_type=jnp.float32
    )
    grad_u = lax.dot_general(
        row_slices, incoming[1], contract_rows, preferred_element_type=jnp.float32
    )
    return (grad_g.astype(jnp.bfloat16), grad_u.astype(jnp.bfloat16), hidden, cand_weight)


def solution(mesh):
    placed = (
        P("dp", "mp"),
        P(None, "mp"),
        P(None, "mp"),
        P("mp"),
        P(),
        P(),
        P("dp", "mp"),
        P("dp", "mp"),
        P("dp", "mp"),
    )
    return jax.shard_map(
        on_device,
        mesh=mesh,
        in_specs=placed,
        out_specs=(P("dp", "mp"), P("dp", "mp"), P("dp", "mp"), P("dp")),
        check_vma=False,
    )
```

```python
import jax
import jax.numpy as jnp
from jax import lax
from jax.sharding import PartitionSpec as P


def gather_by_a2a(x, axis_name, axis):
    parts = lax.psum(1, axis_name)
    stacked = lax.all_to_all(
        jnp.broadcast_to(x[None], (parts,) + x.shape), axis_name, split_axis=0, concat_axis=0, tiled=True
    )
    stacked = jnp.moveaxis(stacked, 0, axis)
    shape = list(x.shape)
    shape[axis] *= parts
    return stacked.reshape(shape)


def on_device(candidates, hold_gate, hold_up, probe, chosen, counts, gate_w, up_w, cotangent):
    cand_dev = candidates.shape[0]
    shards = chosen.shape[0]
    slots = chosen.shape[1]
    width = candidates.shape[1]
    ff = gate_w.shape[1]
    merged = lax.all_gather(jnp.concatenate([candidates, gate_w], axis=1), "dp", axis=0, tiled=True)
    all_cands = merged[:, :width]
    full_w = (merged[:, width:], lax.all_gather(up_w, "dp", axis=0, tiled=True))
    own_index = lax.axis_index("dp")
    source = chosen // cand_dev
    local_row = (chosen % cand_dev).reshape(-1)
    valid = jnp.arange(slots, dtype=jnp.int32)[None, :] < counts[:, None]
    usable = (valid & (source == own_index)).reshape(-1)
    onehot = (
        (local_row[:, None] == jnp.arange(cand_dev, dtype=jnp.int32)[None, :]) & usable[:, None]
    ).astype(jnp.bfloat16)
    own_chosen = lax.dynamic_index_in_dim(chosen, own_index, 0, keepdims=False)
    own_valid = lax.dynamic_index_in_dim(valid, own_index, 0, keepdims=False)
    own_onehot = (
        (own_chosen[:, None] == jnp.arange(all_cands.shape[0], dtype=jnp.int32)[None, :]) & own_valid[:, None]
    ).astype(jnp.bfloat16)
    row_slab = jnp.dot(own_onehot, all_cands, preferred_element_type=jnp.float32).astype(jnp.bfloat16)
    row_x = gather_by_a2a(row_slab, "mp", 1)
    parts = lax.psum(1, "dp")
    row_blocks = row_x.reshape(row_x.shape[0], parts, -1).transpose(1, 0, 2)
    row_slices = lax.all_to_all(row_blocks, "dp", split_axis=0, concat_axis=0, tiled=True)
    row_slices = row_slices.reshape(-1, row_blocks.shape[2])

    incoming = gather_by_a2a(candidates, "mp", 1)
    hold_g = jnp.dot(incoming, hold_gate, preferred_element_type=jnp.float32)
    hold_u = jnp.dot(incoming, hold_up, preferred_element_type=jnp.float32)
    partial_score = jnp.sum(jax.nn.silu(hold_g) * hold_u * probe[None, :], axis=1)
    score = jnp.sum(gather_by_a2a(partial_score[None, :], "mp", 0), axis=0)
    cand_weight = jax.nn.sigmoid(score)
    picked_weight = jnp.dot(
        onehot, cand_weight.astype(jnp.bfloat16)[:, None], preferred_element_type=jnp.float32
    ).astype(jnp.bfloat16).reshape(shards, slots)
    arrived_weight = lax.all_to_all(picked_weight, "dp", split_axis=0, concat_axis=0, tiled=True)
    row_weight = jnp.sum(arrived_weight.astype(jnp.float32), axis=0)

    gate = jnp.dot(row_x, full_w[0], preferred_element_type=jnp.float32)
    up = jnp.dot(row_x, full_w[1], preferred_element_type=jnp.float32)
    hidden = (jax.nn.silu(gate) * up).astype(jnp.bfloat16)
    back = cotangent.astype(jnp.float32) * row_weight[:, None]
    sig = jax.nn.sigmoid(gate)
    d_up = (back * gate * sig).astype(jnp.bfloat16)
    d_gate = (back * up * sig * (1.0 + gate * (1.0 - sig))).astype(jnp.bfloat16)
    contract_rows = (((0,), (0,)), ((), ()))
    d_both, row_slices = lax.optimization_barrier((jnp.stack([d_gate, d_up]), row_slices))
    both_d = lax.all_gather(d_both, "dp", axis=1, tiled=True)
    incoming = (both_d[0], both_d[1])
    grad_g = lax.dot_general(
        row_slices, incoming[0], contract_rows, preferred_element_type=jnp.float32
    )
    grad_u = lax.dot_general(
        row_slices, incoming[1], contract_rows, preferred_element_type=jnp.float32
    )
    return (grad_g.astype(jnp.bfloat16), grad_u.astype(jnp.bfloat16), hidden, cand_weight)


def solution(mesh):
    placed = (
        P("dp", "mp"),
        P(None, "mp"),
        P(None, "mp"),
        P("mp"),
        P(),
        P(),
        P("dp", "mp"),
        P("dp", "mp"),
        P("dp", "mp"),
    )
    return jax.shard_map(
        on_device,
        mesh=mesh,
        in_specs=placed,
        out_specs=(P("dp", "mp"), P("dp", "mp"), P("dp", "mp"), P("dp")),
        check_vma=False,
    )
```

```python
import jax
import jax.numpy as jnp
from jax import lax
from jax.sharding import PartitionSpec as P


def gather_by_a2a(x, axis_name, axis):
    parts = lax.psum(1, axis_name)
    stacked = lax.all_to_all(
        jnp.broadcast_to(x[None], (parts,) + x.shape), axis_name, split_axis=0, concat_axis=0, tiled=True
    )
    stacked = jnp.moveaxis(stacked, 0, axis)
    shape = list(x.shape)
    shape[axis] *= parts
    return stacked.reshape(shape)


def on_device(candidates, hold_gate, hold_up, probe, chosen, counts, gate_w, up_w, cotangent):
    cand_dev = candidates.shape[0]
    shards = chosen.shape[0]
    slots = chosen.shape[1]
    width = candidates.shape[1]
    ff = gate_w.shape[1]
    split = ff // 2
    merged = lax.all_gather(jnp.concatenate([candidates, gate_w[:, :split]], axis=1), "dp", axis=0, tiled=True)
    rest = lax.all_gather(jnp.concatenate([gate_w[:, split:], up_w], axis=1), "dp", axis=0, tiled=True)
    all_cands = merged[:, :width]
    full_w = ((merged[:, width:], rest[:, :ff - split]), rest[:, ff - split:])
    own_index = lax.axis_index("dp")
    source = chosen // cand_dev
    local_row = (chosen % cand_dev).reshape(-1)
    valid = jnp.arange(slots, dtype=jnp.int32)[None, :] < counts[:, None]
    usable = (valid & (source == own_index)).reshape(-1)
    onehot = (
        (local_row[:, None] == jnp.arange(cand_dev, dtype=jnp.int32)[None, :]) & usable[:, None]
    ).astype(jnp.bfloat16)
    own_chosen = lax.dynamic_index_in_dim(chosen, own_index, 0, keepdims=False)
    own_valid = lax.dynamic_index_in_dim(valid, own_index, 0, keepdims=False)
    own_onehot = (
        (own_chosen[:, None] == jnp.arange(all_cands.shape[0], dtype=jnp.int32)[None, :]) & own_valid[:, None]
    ).astype(jnp.bfloat16)
    row_slab = jnp.dot(own_onehot, all_cands, preferred_element_type=jnp.float32).astype(jnp.bfloat16)
    row_x = gather_by_a2a(row_slab, "mp", 1)
    parts = lax.psum(1, "dp")
    row_blocks = row_x.reshape(row_x.shape[0], parts, -1).transpose(1, 0, 2)
    row_slices = lax.all_to_all(row_blocks, "dp", split_axis=0, concat_axis=0, tiled=True)
    row_slices = row_slices.reshape(-1, row_blocks.shape[2])

    incoming = gather_by_a2a(candidates, "mp", 1)
    hold_g = jnp.dot(incoming, hold_gate, preferred_element_type=jnp.float32)
    hold_u = jnp.dot(incoming, hold_up, preferred_element_type=jnp.float32)
    partial_score = jnp.sum(jax.nn.silu(hold_g) * hold_u * probe[None, :], axis=1)
    score = jnp.sum(gather_by_a2a(partial_score[None, :], "mp", 0), axis=0)
    cand_weight = jax.nn.sigmoid(score)
    picked_weight = jnp.dot(
        onehot, cand_weight.astype(jnp.bfloat16)[:, None], preferred_element_type=jnp.float32
    ).astype(jnp.bfloat16).reshape(shards, slots)
    arrived_weight = lax.all_to_all(picked_weight, "dp", split_axis=0, concat_axis=0, tiled=True)
    row_weight = jnp.sum(arrived_weight.astype(jnp.float32), axis=0)

    gate = jnp.concatenate(
        [jnp.dot(row_x, part, preferred_element_type=jnp.float32) for part in full_w[0]], axis=1
    )
    up = jnp.dot(row_x, full_w[1], preferred_element_type=jnp.float32)
    hidden = (jax.nn.silu(gate) * up).astype(jnp.bfloat16)
    back = cotangent.astype(jnp.float32) * row_weight[:, None]
    sig = jax.nn.sigmoid(gate)
    d_up = (back * gate * sig).astype(jnp.bfloat16)
    d_gate = (back * up * sig * (1.0 + gate * (1.0 - sig))).astype(jnp.bfloat16)
    contract_rows = (((0,), (0,)), ((), ()))
    d_both, row_slices = lax.optimization_barrier((jnp.concatenate([d_gate, d_up], axis=1), row_slices))
    both_d = lax.all_gather(d_both, "dp", axis=0, tiled=True)
    incoming = (both_d[:, :ff], both_d[:, ff:])
    grad_g = lax.dot_general(
        row_slices, incoming[0], contract_rows, preferred_element_type=jnp.float32
    )
    grad_u = lax.dot_general(
        row_slices, incoming[1], contract_rows, preferred_element_type=jnp.float32
    )
    return (grad_g.astype(jnp.bfloat16), grad_u.astype(jnp.bfloat16), hidden, cand_weight)


def solution(mesh):
    placed = (
        P("dp", "mp"),
        P(None, "mp"),
        P(None, "mp"),
        P("mp"),
        P(),
        P(),
        P("dp", "mp"),
        P("dp", "mp"),
        P("dp", "mp"),
    )
    return jax.shard_map(
        on_device,
        mesh=mesh,
        in_specs=placed,
        out_specs=(P("dp", "mp"), P("dp", "mp"), P("dp", "mp"), P("dp")),
        check_vma=False,
    )
```

```python
import jax
import jax.numpy as jnp
from jax import lax
from jax.sharding import PartitionSpec as P


def gather_by_a2a(x, axis_name, axis):
    parts = lax.psum(1, axis_name)
    stacked = lax.all_to_all(
        jnp.broadcast_to(x[None], (parts,) + x.shape), axis_name, split_axis=0, concat_axis=0, tiled=True
    )
    stacked = jnp.moveaxis(stacked, 0, axis)
    shape = list(x.shape)
    shape[axis] *= parts
    return stacked.reshape(shape)


def on_device(candidates, hold_gate, hold_up, probe, chosen, counts, gate_w, up_w, cotangent):
    cand_dev = candidates.shape[0]
    shards = chosen.shape[0]
    slots = chosen.shape[1]
    width = candidates.shape[1]
    ff = gate_w.shape[1]
    merged = lax.all_gather(jnp.concatenate([candidates, gate_w], axis=1), "dp", axis=0, tiled=True)
    all_cands = merged[:, :width]
    full_w = (merged[:, width:], lax.all_gather(up_w, "dp", axis=0, tiled=True))
    own_index = lax.axis_index("dp")
    source = chosen // cand_dev
    local_row = (chosen % cand_dev).reshape(-1)
    valid = jnp.arange(slots, dtype=jnp.int32)[None, :] < counts[:, None]
    usable = (valid & (source == own_index)).reshape(-1)
    onehot = (
        (local_row[:, None] == jnp.arange(cand_dev, dtype=jnp.int32)[None, :]) & usable[:, None]
    ).astype(jnp.bfloat16)
    own_chosen = lax.dynamic_index_in_dim(chosen, own_index, 0, keepdims=False)
    own_valid = lax.dynamic_index_in_dim(valid, own_index, 0, keepdims=False)
    own_onehot = (
        (own_chosen[:, None] == jnp.arange(all_cands.shape[0], dtype=jnp.int32)[None, :]) & own_valid[:, None]
    ).astype(jnp.bfloat16)
    row_slab = jnp.dot(own_onehot, all_cands, preferred_element_type=jnp.float32).astype(jnp.bfloat16)
    row_x = gather_by_a2a(row_slab, "mp", 1)
    parts = lax.psum(1, "dp")
    row_blocks = row_x.reshape(row_x.shape[0], parts, -1).transpose(1, 0, 2)
    row_slices = lax.all_to_all(row_blocks, "dp", split_axis=0, concat_axis=0, tiled=True)
    row_slices = row_slices.reshape(-1, row_blocks.shape[2])

    incoming = gather_by_a2a(candidates, "mp", 1)
    hold_g = jnp.dot(incoming, hold_gate, preferred_element_type=jnp.float32)
    hold_u = jnp.dot(incoming, hold_up, preferred_element_type=jnp.float32)
    partial_score = jnp.sum(jax.nn.silu(hold_g) * hold_u * probe[None, :], axis=1)
    score = jnp.sum(gather_by_a2a(partial_score[None, :], "mp", 0), axis=0)
    cand_weight = jax.nn.sigmoid(score)
    picked_weight = jnp.dot(
        onehot, cand_weight.astype(jnp.bfloat16)[:, None], preferred_element_type=jnp.float32
    ).astype(jnp.bfloat16).reshape(shards, slots)
    arrived_weight = lax.all_to_all(picked_weight, "dp", split_axis=0, concat_axis=0, tiled=True)
    row_weight = jnp.sum(arrived_weight.astype(jnp.float32), axis=0)

    gate = jnp.dot(row_x, full_w[0], preferred_element_type=jnp.float32)
    up = jnp.dot(row_x, full_w[1], preferred_element_type=jnp.float32)
    hidden = (jax.nn.silu(gate) * up).astype(jnp.bfloat16)
    back = cotangent.astype(jnp.float32) * row_weight[:, None]
    sig = jax.nn.sigmoid(gate)
    d_up = (back * gate * sig).astype(jnp.bfloat16)
    d_gate = (back * up * sig * (1.0 + gate * (1.0 - sig))).astype(jnp.bfloat16)
    contract_rows = (((0,), (0,)), ((), ()))
    d_both, row_slices = lax.optimization_barrier((jnp.concatenate([d_gate, d_up], axis=1), row_slices))
    both_d = lax.all_gather(d_both, "dp", axis=0, tiled=True)
    grads = lax.dot_general(
        row_slices, both_d, contract_rows, preferred_element_type=jnp.float32
    ).astype(jnp.bfloat16)
    return (grads[:, :ff], grads[:, ff:], hidden, cand_weight)


def solution(mesh):
    placed = (
        P("dp", "mp"),
        P(None, "mp"),
        P(None, "mp"),
        P("mp"),
        P(),
        P(),
        P("dp", "mp"),
        P("dp", "mp"),
        P("dp", "mp"),
    )
    return jax.shard_map(
        on_device,
        mesh=mesh,
        in_specs=placed,
        out_specs=(P("dp", "mp"), P("dp", "mp"), P("dp", "mp"), P("dp")),
        check_vma=False,
    )
```
